128 devices in a mesh: row: 8 (over z, core), col: 16 (over y, x).
Axes of the slice: x: 4, y: 4, z: 4, core: 2. Of those that a mesh axis runs over, the one named last changes fastest.
Arguments:
- tiles: bfloat16 [16384, 128, 128], P(('row', 'col')), may hold values from -6 to 6
- tile_target: int32 [16384, 1], P(('row', 'col')), may hold values from 0 to 127; in each aligned block of 128 rows (0 to 127, 128 to 255, ...) at most 2 rows name the same one
- tile_place: int32 [16384], P(('row', 'col')), may hold values from 0 to 95
- density: bfloat16 [8192, 16384], P('col', 'row'), may hold values from -0.125 to 0.125
Outputs:
- contracted: bfloat16 [49152, 16384], P('col', 'row')
The draws below stay inside these ranges and needn't reach their ends.
Inputs may be any that keep to these rules, and one draw needn't show every extreme that they name: `tile_target`: among the tiles of one device, at most 2 name the same grid position, and some device has exactly 2 tiles for one position.
All inputs are finite; a program needn't handle non-finite values.
Results may differ from the reference program's by a relative error of at most 0.0046.
Values may be sent and summed in bfloat16 or wider, within the bound.
A program may use at most 256 MiB of HBM per device.

```python
import math
import jax
import jax.numpy as jnp
import numpy as np
from jax import lax

BLOCK = 128
TILES_DEV = 128
ROW_BLOCKS_DEV = 24
K_BLOCKS = 4
COL_BLOCKS = 16
STEPS = 4
CAP = 2
POSITIONS = 96
TILES = 16384
SLAB_ROWS = 8192
OUT_COLS = 16384
N_ROW = 8
N_COL = 16
DEVICES = 128


def set_ends(entries, stream_key, smallest, top_value):
    spot = [jax.random.randint(jax.random.fold_in(stream_key, axis), (), 0, length) for axis, length in enumerate(entries.shape)]
    longest = entries.shape.index(max(entries.shape))
    beside = spot[:longest] + [(spot[longest] + 1) % entries.shape[longest]] + spot[longest + 1:]
    return entries.at[tuple(spot)].set(smallest).at[tuple(beside)].set(top_value)


def steps_of(own_key, extent, split, least, top_value):
    gain, own = 1.0, jax.random.fold_in(own_key, 6)
    for axis_at, parts in split:
        draws = jnp.exp(jax.random.uniform(jax.random.fold_in(own, axis_at), (parts,), jnp.float32, least / len(split), top_value / len(split)))
        gain = gain * jnp.repeat(draws, extent[axis_at] // parts).reshape([-1 if axis == axis_at else 1 for axis in range(len(extent))])
    return gain


def routed_block(key, own, number, rows, number_of, top, limit, lean):
    order = jax.random.permutation(key, number_of)
    crowded, usual = shares(number_of, rows * top, limit, lean, True), shares(number_of, rows * top, limit, lean, False)
    places = jnp.arange(number_of)

    def named(tallies, rotation):
        used = int((tallies > 0).sum())
        fixed = max(1, used // 4)
        shifted = fixed + (places - fixed + rotation * (used - fixed)) % max(1, number_of - fixed)
        return jnp.zeros((number_of,), jnp.int32).at[order[jnp.where(places < fixed, places, shifted)]].set(jnp.asarray(tallies, jnp.int32))

    tallies = jnp.where(number % 4 == 0, named(crowded, number // 4), named(usual, number - number // 4 - 1))
    mixed = jax.random.permutation(jax.random.fold_in(own, 3), number_of)
    giver, receiver = mixed[0:number_of // 2 * 2:2], mixed[1:number_of // 2 * 2:2]
    margin = jnp.minimum(tallies[giver] - 1, limit - tallies[receiver]) // 2
    margin = jnp.where((giver == order[0]) | (receiver == order[0]) | (tallies[receiver] == 0), 0, jnp.maximum(margin, 0))
    shifted = jax.random.randint(jax.random.fold_in(own, 4), (number_of // 2,), 0, 1 << 20) % (margin + 1)
    tallies = tallies.at[giver].add(-shifted).at[receiver].add(shifted)
    members = jnp.searchsorted(jnp.cumsum(tallies), jnp.arange(rows * top), side="right").astype(jnp.int32)
    listing = members.reshape(top, rows).T
    listing = listing[jax.random.permutation(jax.random.fold_in(own, 1), rows)]
    rotation = jax.random.randint(jax.random.fold_in(own, 2), (rows, 1), 0, top)
    return jnp.take_along_axis(listing, (jnp.arange(top)[None, :] + rotation) % top, axis=1)


def shares(amount, total, limit, lean, full):
    portions = [(1 << 20) // math.isqrt(standing ** lean) + 1 for standing in range(1, amount + 1)]
    largest = limit if full else min(limit, max(-(-total // amount), total * portions[0] // sum(portions)))
    least = 1 if total - largest >= amount - 1 else 0
    counts, spare = [largest] + [least] * (amount - 1), total - largest - least * (amount - 1)
    while spare > 0:
        movable = [i for i in range(1, amount) if counts[i] < largest] or [i for i in range(1, amount) if counts[i] < limit]
        mass, left = sum([portions[i] for i in movable]), spare
        for i in movable:
            extra = min(limit - counts[i], max(1, left * portions[i] // mass), spare)
            counts[i] = counts[i] + extra
            spare = spare - extra
    return np.array(counts)


def bell_draw(own_key, dims, spread, bound, split=(), held_as=jnp.bfloat16):
    loudness = steps_of(own_key, dims, split, -0.22, 0.18) if split else 1.0
    array = jax.random.normal(own_key, dims, jnp.float32) * spread * loudness
    return jnp.minimum(jnp.maximum(array, -bound), bound).astype(held_as)


def setup_inputs(seed: int = 0) -> dict:
    splits = jax.random.split(jax.random.key(seed), 5)
    tiles = bell_draw(splits[0], (TILES, BLOCK, BLOCK), 1.0, 6.0, ((0, 128),))
    tile_target_keys = jax.random.split(jax.random.fold_in(splits[1], 1), TILES // TILES_DEV)
    tile_target_turns = jax.random.permutation(jax.random.fold_in(splits[1], 3), TILES // TILES_DEV)
    tile_target = jax.vmap(lambda own, number: routed_block(jax.random.fold_in(splits[1], 2), own, number, TILES_DEV, DEVICES, 1, CAP, 2))(tile_target_keys, tile_target_turns).reshape((TILES, 1))
    tile_place = set_ends(jax.random.randint(splits[2], (TILES,), 0, POSITIONS), jax.random.fold_in(splits[2], 1), 0, POSITIONS - 1).astype(jnp.int32)
    density = bell_draw(splits[3], (SLAB_ROWS, OUT_COLS), (STEPS * K_BLOCKS * BLOCK) ** -0.5, 0.125, ((0, 16), (1, 8)))
    return dict(tiles=tiles, tile_target=tile_target, tile_place=tile_place, density=density)


def reference(tiles, tile_target, tile_place, density):
    tile_size = BLOCK
    segment_ids = (tile_target[:, 0] * POSITIONS + tile_place).astype(jnp.int32)
    summed = jax.ops.segment_sum(tiles.astype(jnp.float32), segment_ids, num_segments=DEVICES * POSITIONS)
    panels = summed.reshape(N_ROW, N_COL, ROW_BLOCKS_DEV, K_BLOCKS, tile_size, tile_size)
    panels = panels.transpose(0, 1, 2, 4, 3, 5).reshape(N_ROW, N_COL, ROW_BLOCKS_DEV * tile_size, K_BLOCKS * tile_size)
    panels = panels.astype(jnp.bfloat16)
    slabs = density.reshape(N_COL, K_BLOCKS * tile_size, N_ROW, COL_BLOCKS * tile_size).transpose(0, 2, 1, 3)

    def one_block(flat_index):
        row_index = flat_index // N_COL
        col_index = flat_index % N_COL
        total = jnp.zeros((ROW_BLOCKS_DEV * tile_size, COL_BLOCKS * tile_size), jnp.float32)
        for offset in range(STEPS):
            left = panels[(row_index + offset) % N_ROW, col_index]
            right = slabs[(col_index + offset) % N_COL, row_index]
            total = total + jnp.dot(left, right, preferred_element_type=jnp.float32)
        return total.astype(jnp.bfloat16)

    blocks = lax.map(one_block, jnp.arange(DEVICES, dtype=jnp.int32))
    blocks = blocks.reshape(N_ROW, N_COL, ROW_BLOCKS_DEV * tile_size, COL_BLOCKS * tile_size)
    return blocks.transpose(1, 2, 0, 3).reshape(N_COL * ROW_BLOCKS_DEV * tile_size, N_ROW * COL_BLOCKS * tile_size)
```

```python
import functools

import jax
import jax.numpy as jnp
from jax import lax
from jax.experimental import pallas as pl
from jax.experimental.pallas import tpu as pltpu
from jax.sharding import PartitionSpec as P

K_BLOCKS = 4
POSITIONS = 96
CAP = 2
CHUNKS = 3


def permuted(value, axis, pairs):
    return lax.ppermute(value, axis, pairs)


def shifted(value, axis, steps):
    count = lax.axis_size(axis)
    return permuted(value, axis, [(s, (s + steps) % count) for s in range(count)])


def pack_kernel(shift, devices, target_ref, place_ref, tiles_ref, send_ref, places_ref, held, used, slots, in_sem, out_sem):
    tile_count = tiles_ref.shape[0]
    load = pltpu.make_async_copy(tiles_ref, held, in_sem)
    load.start()

    @pl.loop(0, devices)
    def _(d):
        used[d] = 0
        for c in range(CAP):
            places_ref[d * CAP + c] = -1

    @pl.loop(0, tile_count)
    def _(t):
        dest = lax.rem(target_ref[t] + shift, devices)
        rank = used[dest]
        used[dest] = rank + 1
        slot = dest * CAP + rank
        slots[t] = slot
        places_ref[slot] = place_ref[t]

    load.wait()

    @pl.loop(0, tile_count)
    def _(t):
        pltpu.make_async_copy(held.at[t], send_ref.at[slots[t]], out_sem).start()

    pltpu.make_async_copy(held, send_ref.at[pl.ds(0, tile_count)], out_sem).wait()


def pack(tiles, targets, places, shift, devices):
    tile_count, size, _ = tiles.shape
    smem = pl.BlockSpec(memory_space=pltpu.SMEM)
    return pl.pallas_call(
        functools.partial(pack_kernel, shift, devices),
        out_shape=(
            jax.ShapeDtypeStruct((devices * CAP, size, size), tiles.dtype),
            jax.ShapeDtypeStruct((devices * CAP,), jnp.int32),
        ),
        in_specs=[smem, smem, pl.BlockSpec(memory_space=pl.ANY)],
        out_specs=(pl.BlockSpec(memory_space=pl.ANY), smem),
        scratch_shapes=[
            pltpu.VMEM(tiles.shape, tiles.dtype),
            pltpu.SMEM((devices,), jnp.int32),
            pltpu.SMEM((tile_count,), jnp.int32),
            pltpu.SemaphoreType.DMA,
            pltpu.SemaphoreType.DMA,
        ],
        name="pack",
    )(targets, places, tiles)


def add_kernel(groups, place_ref, got_ref, panel_ref, held, total, seen, sems):
    slots, size, _ = got_ref.shape
    per = slots // groups

    def copy(g):
        part = pl.ds(g * per, per)
        return pltpu.make_async_copy(got_ref.at[part], held.at[part], sems.at[g])

    for g in range(groups):
        copy(g).start()

    @pl.loop(0, POSITIONS)
    def _(b):
        seen[b] = 0

    for g in range(groups):
        copy(g).wait()

        @pl.loop(g * per, (g + 1) * per)
        def _(s):
            place = place_ref[s]

            @pl.when(place >= 0)
            def _():
                first = seen[place] == 0
                tile = held[s].astype(jnp.float32)

                @pl.when(first)
                def _():
                    total[place] = tile
                    seen[place] = 1

                @pl.when(jnp.logical_not(first))
                def _():
                    total[place] += tile

    @pl.loop(0, POSITIONS // K_BLOCKS)
    def _(r):
        rows = pl.ds(pl.multiple_of(r * size, size), size)
        for k in range(K_BLOCKS):
            block = r * K_BLOCKS + k
            value = jnp.where(seen[block] > 0, total[block], 0.0)
            panel_ref[rows, k * size:(k + 1) * size] = value.astype(panel_ref.dtype)


def add_tiles(got, places):
    slots, size, _ = got.shape
    groups = 8
    return pl.pallas_call(
        functools.partial(add_kernel, groups),
        out_shape=jax.ShapeDtypeStruct((POSITIONS // K_BLOCKS * size, K_BLOCKS * size), got.dtype),
        in_specs=[pl.BlockSpec(memory_space=pltpu.SMEM), pl.BlockSpec(memory_space=pl.ANY)],
        out_specs=pl.BlockSpec(memory_space=pltpu.VMEM),
        scratch_shapes=[
            pltpu.VMEM(got.shape, got.dtype),
            pltpu.VMEM((POSITIONS, size, size), jnp.float32),
            pltpu.SMEM((POSITIONS,), jnp.int32),
            pltpu.SemaphoreType.DMA((groups,)),
        ],
        name="add_tiles",
    )(places, got)


def product_kernel(steps, wide, *refs):
    lefts, rights, out_ref = refs[:steps], refs[steps:2 * steps], refs[-1]
    left = jnp.concatenate([ref[...] for ref in lefts], axis=1)
    for n in range(0, out_ref.shape[1], wide):
        right = jnp.concatenate([ref[:, n:n + wide] for ref in rights], axis=0)
        out = jnp.dot(left, right, preferred_element_type=jnp.float32)
        out_ref[:, n:n + wide] = out.astype(out_ref.dtype)


def product(lefts, rights, start, rows_all, out):
    rows, depth = lefts[0].shape
    columns = rights[0].shape[1]
    tall = 256
    steps = len(lefts)
    base = start // tall
    body = functools.partial(product_kernel, steps, 512)
    args = list(lefts) + list(rights)
    specs = [pl.BlockSpec((tall, depth), lambda m: (m, 0))] * steps
    specs += [pl.BlockSpec((depth, columns), lambda m: (0, 0), pipeline_mode=pl.Buffered(1))] * steps
    aliases = {}
    if out is not None:
        args.append(out)
        specs.append(pl.BlockSpec(memory_space=pl.ANY))
        aliases = {2 * steps: 0}
    return pl.pallas_call(
        body,
        grid=(rows // tall,),
        out_shape=jax.ShapeDtypeStruct((rows_all, columns), jnp.bfloat16),
        in_specs=specs,
        out_specs=pl.BlockSpec((tall, columns), lambda m: (m + base, 0)),
        input_output_aliases=aliases,
        cost_estimate=pl.CostEstimate(
            flops=2 * rows * columns * depth * steps,
            bytes_accessed=2 * (rows * columns + steps * depth * (rows + columns)),
            transcendentals=0,
        ),
        name="product",
    )(*args)


def on_device(tiles, tile_target, tile_place, density):
    row_count = lax.axis_size("row")
    col_count = lax.axis_size("col")
    devices = row_count * col_count
    size = tiles.shape[1]
    send, places = pack(tiles, tile_target[:, 0], tile_place, devices - col_count, devices)
    got = lax.all_to_all(send.reshape(devices, CAP, size, size), ("row", "col"), split_axis=0, concat_axis=0, tiled=True)
    got_places = lax.all_to_all(places.reshape(devices, CAP), ("row", "col"), split_axis=0, concat_axis=0, tiled=True)
    one = shifted(density, "col", -1)
    three = shifted(density, "col", -3)
    half = density.shape[1] // 2
    two = jnp.concatenate([shifted(one[:, :half], "col", -1), shifted(three[:, half:], "col", 1)], axis=1)
    rights = (density, one, two, three)

    panel = add_tiles(got.reshape(devices * CAP, size, size), got_places.reshape(devices * CAP))
    even = lax.axis_index("row") % 2 == 0
    swap = [(s, s ^ 1) for s in range(row_count)]
    rows_all = panel.shape[0]
    rows = rows_all // CHUNKS
    lefts = []
    for c in range(CHUNKS):
        own = panel[c * rows:(c + 1) * rows]
        last = shifted(own, "row", -2)
        first = shifted(own, "row", 1)
        mid = permuted(jnp.where(even, last, own), "row", swap)
        lefts.append((first, own, mid, last))
    out = None
    for c in range(CHUNKS):
        out = product(lefts[c], rights, c * rows, rows_all, out)
    return out


def solution(mesh):
    in_specs = (
        P(("row", "col"), None, None),
        P(("row", "col"), None),
        P(("row", "col")),
        P("col", "row"),
    )
    return jax.shard_map(on_device, mesh=mesh, in_specs=in_specs, out_specs=P("col", "row"), check_vma=False)
```
